128 devices in a mesh: dp: 2 (over core), expert: 64 (over z, y, x).
Axes of the slice: x: 4, y: 4, z: 4, core: 2. Of those that a mesh axis runs over, the one named last changes fastest.
Arguments:
- patches: bfloat16 [10240, 2048], P('expert', 'dp'), may hold values from -6 to 6
- expert_ids: int32 [10240, 2], P('expert'), may hold values from 0 to 63, all different within a row; in each aligned block of 160 rows (0 to 159, 160 to 319, ...) at most 15 rows name the same one
- gate_probs: float32 [10240, 2], P('expert'), may hold values from 0.1 to 1
- out_grad: bfloat16 [10240, 2048], P('expert', 'dp'), may hold values from -6 to 6
- w_gate: bfloat16 [64, 2048, 1024], P('expert', None, 'dp'), may hold values from -0.125 to 0.125
- w_up: bfloat16 [64, 2048, 1024], P('expert', None, 'dp'), may hold values from -0.125 to 0.125
- w_down: bfloat16 [64, 1024, 2048], P('expert', None, 'dp'), may hold values from -0.1875 to 0.1875
Outputs:
- mixed: bfloat16 [10240, 2048], P('expert', 'dp')
- patch_grad: bfloat16 [10240, 2048], P('expert', 'dp')
- w_gate_grad: bfloat16 [64, 2048, 1024], P('expert', None, 'dp')
- w_up_grad: bfloat16 [64, 2048, 1024], P('expert', None, 'dp')
- w_down_grad: bfloat16 [64, 1024, 2048], P('expert', None, 'dp')
The draws below stay inside these ranges and needn't reach their ends.
Inputs may be any that keep to these rules, and one draw needn't show every extreme that they name: `expert_ids`: the 2 experts of a row differ. Among the 160 rows of one device no expert is named by more than 15 rows, and on some device an expert is named by exactly 15; on every device every expert is named by at least one row.
All inputs are finite; a program needn't handle non-finite values.
Results may differ from the reference program's by a relative error of at most 0.0065.
Values may be sent and summed in bfloat16 or wider, within the bound.
No kernel may reach another device: no remote copies, remote signals or barrier semaphores. Data moves between devices by JAX's collectives and lax.ppermute only.
A program may use at most 128 MiB of HBM per device.

```python
import math
import jax
import jax.numpy as jnp
import numpy as np
from jax import lax

D = 2048
HIDDEN_SIZE = 1024
TOP = 2
TOK_DEV = 160
EXPERTS = 64
CAP = 15
TOKENS = 10240


def steps_of(stream_key, extent, cuts, least, top_value):
    gain = 1.0
    for dim, parts in cuts:
        heights = jax.random.uniform(jax.random.fold_in(jax.random.fold_in(stream_key, 6), dim), (parts,), jnp.float32, least / len(cuts), top_value / len(cuts))
        gain = gain * jnp.repeat(jnp.exp(heights), extent[dim] // parts).reshape((-1,) + (1,) * (len(extent) - 1 - dim))
    return gain


def routed_block(own_key, own, number, rows, amount, top, reach, lean):
    sequence = jax.random.permutation(own_key, amount)
    heavy_load, ordinary = shares(amount, rows * top, reach, lean, True), shares(amount, rows * top, reach, lean, False)
    places = jnp.arange(amount)

    def named(sizes, offset_by):
        used = int((sizes > 0).sum())
        fixed = max(1, used // 4)
        moved = fixed + (places - fixed + offset_by * (used - fixed)) % max(1, amount - fixed)
        return jnp.zeros((amount,), jnp.int32).at[sequence[jnp.where(places < fixed, places, moved)]].set(jnp.asarray(sizes, jnp.int32))

    sizes = jnp.where(number % 4 == 0, named(heavy_load, number // 4), named(ordinary, number - number // 4 - 1))
    mixed = jax.random.permutation(jax.random.fold_in(own, 3), amount)
    source_of, taker = mixed[0:amount // 2 * 2:2], mixed[1:amount // 2 * 2:2]
    margin = jnp.minimum(sizes[source_of] - 1, reach - sizes[taker]) // 2
    margin = jnp.where((source_of == sequence[0]) | (taker == sequence[0]) | (sizes[taker] == 0), 0, jnp.maximum(margin, 0))
    moved = jax.random.randint(jax.random.fold_in(own, 4), (amount // 2,), 0, 1 << 20) % (margin + 1)
    sizes = sizes.at[source_of].add(-moved).at[taker].add(moved)
    members = jnp.searchsorted(jnp.cumsum(sizes), jnp.arange(rows * top), side="right").astype(jnp.int32)
    grid = members.reshape(top, rows).T
    grid = grid[jax.random.permutation(jax.random.fold_in(own, 1), rows)]
    offset_by = jax.random.randint(jax.random.fold_in(own, 2), (rows, 1), 0, top)
    return jnp.take_along_axis(grid, (jnp.arange(top)[None, :] + offset_by) % top, axis=1)


def shares(number_of, total, bound, skew, full):
    weights = [(1 << 20) // math.isqrt(rank ** skew) + 1 for rank in range(1, number_of + 1)]
    largest = bound if full else min(bound, max(-(-total // number_of), total * weights[0] // sum(weights)))
    least = 1 if total - largest >= number_of - 1 else 0
    counts, spare = [largest] + [least] * (number_of - 1), total - largest - least * (number_of - 1)
    while spare > 0:
        movable = [i for i in range(1, number_of) if counts[i] < largest] or [i for i in range(1, number_of) if counts[i] < bound]
        pool, remaining = sum([weights[i] for i in movable]), spare
        for i in movable:
            more = min(bound - counts[i], max(1, remaining * weights[i] // pool), spare)
            counts[i] = counts[i] + more
            spare = spare - more
    return np.array(counts)


def gaussian(own_key, shape, width, most, split=(), kind=jnp.bfloat16):
    entries = jax.random.normal(own_key, shape, jnp.float32) * width
    if len(split) > 0:
        entries = steps_of(own_key, shape, split, -0.22, 0.18) * entries
    return jnp.clip(entries, min=-most, max=most).astype(kind)


def setup_inputs(seed: int = 0) -> dict:
    key_list = jax.random.split(jax.random.key(seed), 8)
    patches = gaussian(key_list[0], (TOKENS, D), 1.0, 6.0, ((0, 64), (1, 2)))
    expert_ids_keys = jax.random.split(jax.random.fold_in(key_list[1], 1), TOKENS // TOK_DEV)
    expert_ids_turns = jax.random.permutation(jax.random.fold_in(key_list[1], 3), TOKENS // TOK_DEV)
    expert_ids = jax.vmap(lambda own, number: routed_block(jax.random.fold_in(key_list[1], 2), own, number, TOK_DEV, EXPERTS, TOP, CAP, 2))(expert_ids_keys, expert_ids_turns).reshape((TOKENS, TOP))
    gate_probs = jnp.clip(0.1 + 0.9 * jax.random.uniform(key_list[2], (TOKENS, TOP), jnp.float32) ** steps_of(key_list[2], (TOKENS, TOP), ((0, 64),), -0.2, 0.2), 0.1, 1.0)
    out_grad = gaussian(key_list[3], (TOKENS, D), 1.0, 6.0, ((0, 64), (1, 2)))
    w_gate = gaussian(key_list[4], (EXPERTS, D, HIDDEN_SIZE), D ** -0.5, 0.125, ((0, 64), (2, 2)))
    w_up = gaussian(key_list[5], (EXPERTS, D, HIDDEN_SIZE), D ** -0.5, 0.125, ((0, 64), (2, 2)))
    w_down = gaussian(key_list[6], (EXPERTS, HIDDEN_SIZE, D), HIDDEN_SIZE ** -0.5, 0.1875, ((0, 64), (2, 2)))
    return {"patches": patches, "expert_ids": expert_ids, "gate_probs": gate_probs, "out_grad": out_grad, "w_gate": w_gate, "w_up": w_up, "w_down": w_down}


def contract_first(left_side, right_side):
    return lax.dot_general(left_side, right_side, (((0,), (0,)), ((), ())), preferred_element_type=jnp.float32)


def contract_last(left_side, right_side):
    return lax.dot_general(left_side, right_side, (((1,), (1,)), ((), ())), preferred_element_type=jnp.float32)


def reference(patches, expert_ids, gate_probs, out_grad, w_gate, w_up, w_down):
    sources = TOKENS // TOK_DEV
    per_expert = sources * CAP
    blocked = expert_ids.reshape(sources, TOK_DEV * TOP).astype(jnp.int32)
    onehot = (blocked[:, :, None] == jnp.arange(EXPERTS, dtype=jnp.int32)[None, None, :]).astype(jnp.int32)
    earlier = jnp.cumsum(onehot, axis=1) - onehot
    ranks = jnp.sum(earlier * onehot, axis=2)
    source_ids = jnp.arange(sources, dtype=jnp.int32)[:, None]
    places = (blocked * per_expert + source_ids * CAP + ranks).reshape(-1).astype(jnp.int32)
    route_rows = (source_ids * TOK_DEV + jnp.arange(TOK_DEV * TOP, dtype=jnp.int32)[None, :] // TOP).reshape(-1).astype(jnp.int32)
    table = jnp.full((EXPERTS * per_expert,), TOKENS, jnp.int32).at[places].set(route_rows)
    route_probs = jnp.zeros((EXPERTS * per_expert,), jnp.float32).at[places].set(gate_probs.reshape(-1).astype(jnp.float32))
    table = table.reshape(EXPERTS, per_expert)
    route_probs = route_probs.reshape(EXPERTS, per_expert)
    padded_rows = jnp.concatenate([patches, jnp.zeros((1, D), patches.dtype)], axis=0)
    padded_grads = jnp.concatenate([out_grad, jnp.zeros((1, D), out_grad.dtype)], axis=0)

    def one_expert(running, inputs):
        rows_at, probs, gate_w, up_w, down_w = inputs
        inputs_e = padded_rows[rows_at]
        gate_pre = jnp.dot(inputs_e, gate_w, preferred_element_type=jnp.float32)
        up_pre = jnp.dot(inputs_e, up_w, preferred_element_type=jnp.float32)
        sigma_gate = jax.nn.sigmoid(gate_pre)
        hidden = (gate_pre * sigma_gate * up_pre).astype(jnp.bfloat16)
        expert_out = jnp.dot(hidden, down_w, preferred_element_type=jnp.float32).astype(jnp.bfloat16)
        slot_grad = (probs[:, None] * padded_grads[rows_at].astype(jnp.float32)).astype(jnp.bfloat16)
        down_grad = contract_first(hidden, slot_grad).astype(jnp.bfloat16)
        hidden_grad = contract_last(slot_grad, down_w)
        gate_grad = (hidden_grad * up_pre * sigma_gate * (1.0 + gate_pre * (1.0 - sigma_gate))).astype(jnp.bfloat16)
        up_grad = (hidden_grad * gate_pre * sigma_gate).astype(jnp.bfloat16)
        gate_wgrad = contract_first(inputs_e, gate_grad).astype(jnp.bfloat16)
        up_wgrad = contract_first(inputs_e, up_grad).astype(jnp.bfloat16)
        route_grad = (contract_last(gate_grad, gate_w) + contract_last(up_grad, up_w)).astype(jnp.bfloat16)
        out_acc, grad_acc = running
        out_acc = out_acc.at[rows_at].add(probs[:, None] * expert_out.astype(jnp.float32))
        grad_acc = grad_acc.at[rows_at].add(route_grad.astype(jnp.float32))
        return (out_acc, grad_acc), (gate_wgrad, up_wgrad, down_grad)

    start_acc = (jnp.zeros((TOKENS + 1, D), jnp.float32), jnp.zeros((TOKENS + 1, D), jnp.float32))
    (out_acc, grad_acc), (gate_wgrads, up_wgrads, down_wgrads) = lax.scan(
        one_expert, start_acc, (table, route_probs, w_gate, w_up, w_down))
    mixed = out_acc[:TOKENS].astype(jnp.bfloat16)
    patch_grad = grad_acc[:TOKENS].astype(jnp.bfloat16)
    return (mixed, patch_grad, gate_wgrads, up_wgrads, down_wgrads)
```

```python
import jax
import jax.numpy as jnp
from jax import lax
from jax.sharding import PartitionSpec as P

F32 = jnp.float32
BF16 = jnp.bfloat16


def dot(left, right, left_dims, right_dims):
    return lax.dot_general(
        left, right, ((left_dims, right_dims), ((), ())), preferred_element_type=F32
    )


def body(patches, expert_ids, gate_probs, out_grad, w_gate, w_up, w_down):
    tok_rows, width_dev = patches.shape
    top_count = expert_ids.shape[1]
    experts = lax.axis_size("expert")
    cores = lax.axis_size("dp")
    core = lax.axis_index("dp")
    hidden_dev = w_gate.shape[2]
    width = w_gate.shape[1]
    per_core = 8
    core_slots = experts * per_core
    slot_count = cores * core_slots

    def swap(value):
        return lax.ppermute(value, "dp", [(0, 1), (1, 0)])

    def exchange(value):
        return lax.all_to_all(
            value.reshape(cores * experts, per_core, width_dev),
            ("dp", "expert"),
            split_axis=0,
            concat_axis=0,
            tiled=True,
        ).reshape(cores, core_slots, width_dev)

    def in_order(mine, other, axis):
        first = jnp.where(core == 0, mine, other)
        second = jnp.where(core == 0, other, mine)
        return first, second

    flat_ids = expert_ids.reshape(-1)
    onehot = (flat_ids[:, None] == jnp.arange(experts, dtype=jnp.int32)[None, :]).astype(F32)
    route_count = tok_rows * top_count
    before = (
        jnp.arange(route_count, dtype=jnp.int32)[:, None]
        > jnp.arange(route_count, dtype=jnp.int32)[None, :]
    ).astype(BF16)
    earlier = dot(before, onehot.astype(BF16), (1,), (0,))
    ranks = jnp.sum(earlier * onehot, axis=1).astype(jnp.int32)
    slots = ((ranks % 2) * core_slots + flat_ids * per_core + ranks // 2).reshape(
        tok_rows, top_count
    )
    positions = jnp.arange(slot_count, dtype=jnp.int32)[:, None]
    hits = [positions == slots[None, :, k] for k in range(top_count)]
    select = (hits[0] | hits[1]).astype(BF16)
    slot_probs = sum(
        jnp.sum(jnp.where(hits[k], gate_probs[None, :, k], 0.0), axis=1, keepdims=True)
        for k in range(top_count)
    )

    sent_rows = dot(select, patches, (1,), (0,)).astype(BF16)
    rows = exchange(sent_rows)
    sent_grads = (dot(select, out_grad, (1,), (0,)) * slot_probs).astype(BF16)
    grads = exchange(sent_grads)

    gate_lo, gate_hi = in_order(w_gate[0], swap(w_gate[0]), 1)
    up_lo, up_hi = in_order(w_up[0], swap(w_up[0]), 1)
    pair_weights = jnp.concatenate([gate_lo, gate_hi, up_lo, up_hi], axis=1)
    down_weights = jnp.stack(in_order(w_down[0], swap(w_down[0]), 1), axis=0)
    hidden_all = cores * hidden_dev

    rows_full = jnp.concatenate([rows[0], rows[1]], axis=1)
    projected = dot(rows_full, pair_weights, (1,), (0,))
    gate_pre = projected[:, :hidden_all]
    up_pre = projected[:, hidden_all:]
    sigma = jax.nn.sigmoid(gate_pre)
    hidden = (gate_pre * sigma * up_pre).astype(BF16)
    expert_out = jnp.stack(
        [dot(hidden, down_weights[i], (1,), (0,)).astype(BF16) for i in range(cores)], axis=0
    )
    back_out = exchange(expert_out).reshape(slot_count, width_dev)

    hidden_grad = sum(dot(grads[i], down_weights[i], (1,), (1,)) for i in range(cores))
    gate_grad = (hidden_grad * up_pre * sigma * (1.0 + gate_pre * (1.0 - sigma))).astype(BF16)
    up_grad = (hidden_grad * gate_pre * sigma).astype(BF16)
    pair_grad = jnp.concatenate([gate_grad, up_grad], axis=1)
    dx_slots = jnp.stack(
        [
            dot(
                pair_grad, pair_weights[i * width_dev : (i + 1) * width_dev], (1,), (1,)
            ).astype(BF16)
            for i in range(cores)
        ],
        axis=0,
    )
    back_grad = exchange(dx_slots).reshape(slot_count, width_dev)

    rows_other = swap(rows_full)
    hidden_other = swap(hidden)
    grads_mine, grads_send = in_order(grads[0], grads[1], 1)
    grads_other = swap(grads_send)
    down_grad = (
        dot(hidden, grads_mine, (0,), (0,)) + dot(hidden_other, grads_other, (0,), (0,))
    ).astype(BF16)

    def share(value):
        return in_order(value[:, :hidden_dev], value[:, hidden_dev:], 1)

    gate_mine, gate_send = share(gate_grad)
    up_mine, up_send = share(up_grad)
    gate_other = swap(gate_send)
    up_other = swap(up_send)

    def row_grad(mine, other):
        return (
            dot(rows_full, mine, (0,), (0,)) + dot(rows_other, other, (0,), (0,))
        ).astype(BF16)

    gate_wgrad = row_grad(gate_mine, gate_other)
    up_wgrad = row_grad(up_mine, up_other)

    picked = [
        dot(hits[k].astype(BF16), back_out, (0,), (0,)) * gate_probs[:, k : k + 1]
        for k in range(top_count)
    ]
    mixed = (picked[0] + picked[1]).astype(BF16)
    patch_grad = dot(select, back_grad, (0,), (0,)).astype(BF16)
    return mixed, patch_grad, gate_wgrad[None], up_wgrad[None], down_grad[None]


def solution(mesh):
    in_specs = (
        P("expert", "dp"),
        P("expert", None),
        P("expert", None),
        P("expert", "dp"),
        P("expert", None, "dp"),
        P("expert", None, "dp"),
        P("expert", None, "dp"),
    )
    out_specs = (
        P("expert", "dp"),
        P("expert", "dp"),
        P("expert", None, "dp"),
        P("expert", None, "dp"),
        P("expert", None, "dp"),
    )
    return jax.shard_map(body, mesh=mesh, in_specs=in_specs, out_specs=out_specs, check_vma=False)
```

```python
import jax
import jax.numpy as jnp
from jax import lax
from jax.sharding import PartitionSpec as P


F32 = jnp.float32
BF16 = jnp.bfloat16


def dot(left, right, left_dims, right_dims):
    return lax.dot_general(
        left, right, ((left_dims, right_dims), ((), ())), preferred_element_type=F32
    )


def body(patches, expert_ids, gate_probs, out_grad, w_gate, w_up, w_down):
    tok_rows, width_dev = patches.shape
    top_count = expert_ids.shape[1]
    experts = lax.axis_size("expert")
    cores = lax.axis_size("dp")
    core = lax.axis_index("dp")
    hidden_dev = w_gate.shape[2]
    per_core = 8
    core_slots = experts * per_core
    slot_count = cores * core_slots

    def swap(value):
        return lax.ppermute(value, "dp", [(0, 1), (1, 0)])

    def exchange(value):
        return lax.all_to_all(
            value.reshape(cores * experts, per_core, width_dev),
            ("dp", "expert"),
            split_axis=0,
            concat_axis=0,
            tiled=True,
        ).reshape(cores, core_slots, width_dev)

    def in_order(mine, other):
        first = jnp.where(core == 0, mine, other)
        second = jnp.where(core == 0, other, mine)
        return first, second

    flat_ids = expert_ids.reshape(-1)
    onehot = (flat_ids[:, None] == jnp.arange(experts, dtype=jnp.int32)[None, :]).astype(F32)
    route_count = tok_rows * top_count
    before = (
        jnp.arange(route_count, dtype=jnp.int32)[:, None]
        > jnp.arange(route_count, dtype=jnp.int32)[None, :]
    ).astype(BF16)
    earlier = dot(before, onehot.astype(BF16), (1,), (0,))
    ranks = jnp.sum(earlier * onehot, axis=1).astype(jnp.int32)
    slots = ((ranks % 2) * core_slots + flat_ids * per_core + ranks // 2).reshape(
        tok_rows, top_count
    )
    positions = jnp.arange(slot_count, dtype=jnp.int32)[:, None]
    hits = [positions == slots[None, :, k] for k in range(top_count)]
    select = (hits[0] | hits[1]).astype(BF16)
    slot_probs = sum(
        jnp.sum(jnp.where(hits[k], gate_probs[None, :, k], 0.0), axis=1, keepdims=True)
        for k in range(top_count)
    )

    sent_rows = dot(select, patches, (1,), (0,)).astype(BF16)
    rows = exchange(sent_rows)
    sent_grads = (dot(select, out_grad, (1,), (0,)) * slot_probs).astype(BF16)
    grads = exchange(sent_grads)

    gate_lo, gate_hi = in_order(w_gate[0], swap(w_gate[0]))
    up_lo, up_hi = in_order(w_up[0], swap(w_up[0]))
    pair_weights = jnp.concatenate([gate_lo, gate_hi, up_lo, up_hi], axis=1)
    down_weights = jnp.stack(in_order(w_down[0], swap(w_down[0])), axis=0)
    hidden_all = cores * hidden_dev

    rows_full = jnp.concatenate([rows[0], rows[1]], axis=1)
    projected = dot(rows_full, pair_weights, (1,), (0,))
    gate_pre = projected[:, :hidden_all]
    up_pre = projected[:, hidden_all:]
    sigma = jax.nn.sigmoid(gate_pre)
    hidden = (gate_pre * sigma * up_pre).astype(BF16)
    projected, hidden = lax.optimization_barrier((projected, hidden))
    gate_pre = projected[:, :hidden_all]
    up_pre = projected[:, hidden_all:]
    sigma = jax.nn.sigmoid(gate_pre)
    expert_out = jnp.stack(
        [dot(hidden, down_weights[i], (1,), (0,)).astype(BF16) for i in range(cores)], axis=0
    )
    back_out = exchange(expert_out).reshape(slot_count, width_dev)

    hidden_grad = sum(dot(grads[i], down_weights[i], (1,), (1,)) for i in range(cores))
    gate_grad = (hidden_grad * up_pre * sigma * (1.0 + gate_pre * (1.0 - sigma))).astype(BF16)
    up_grad = (hidden_grad * gate_pre * sigma).astype(BF16)
    pair_grad = jnp.concatenate([gate_grad, up_grad], axis=1)
    dx_slots = jnp.stack(
        [
            dot(
                pair_grad, pair_weights[i * width_dev : (i + 1) * width_dev], (1,), (1,)
            ).astype(BF16)
            for i in range(cores)
        ],
        axis=0,
    )
    back_grad = exchange(dx_slots).reshape(slot_count, width_dev)

    rows_other = swap(rows_full)
    hidden_other = swap(hidden)
    grads_mine, grads_send = in_order(grads[0], grads[1])
    grads_other = swap(grads_send)
    down_grad = (
        dot(hidden, grads_mine, (0,), (0,)) + dot(hidden_other, grads_other, (0,), (0,))
    ).astype(BF16)

    def share(value):
        return in_order(value[:, :hidden_dev], value[:, hidden_dev:])

    gate_mine, gate_send = share(gate_grad)
    up_mine, up_send = share(up_grad)
    gate_other = swap(gate_send)
    up_other = swap(up_send)

    def row_grad(mine, other):
        return (
            dot(rows_full, mine, (0,), (0,)) + dot(rows_other, other, (0,), (0,))
        ).astype(BF16)

    gate_wgrad = row_grad(gate_mine, gate_other)
    up_wgrad = row_grad(up_mine, up_other)

    picked = [
        dot(hits[k].astype(BF16), back_out, (0,), (0,)) * gate_probs[:, k : k + 1]
        for k in range(top_count)
    ]
    mixed = (picked[0] + picked[1]).astype(BF16)
    patch_grad = dot(select, back_grad, (0,), (0,)).astype(BF16)
    return mixed, patch_grad, gate_wgrad[None], up_wgrad[None], down_grad[None]


def solution(mesh):
    in_specs = (
        P("expert", "dp"),
        P("expert", None),
        P("expert", None),
        P("expert", "dp"),
        P("expert", None, "dp"),
        P("expert", None, "dp"),
        P("expert", None, "dp"),
    )
    out_specs = (
        P("expert", "dp"),
        P("expert", "dp"),
        P("expert", None, "dp"),
        P("expert", None, "dp"),
        P("expert", None, "dp"),
    )

    return jax.shard_map(body, mesh=mesh, in_specs=in_specs, out_specs=out_specs, check_vma=False)
```

```python
import functools

import jax
import jax.numpy as jnp
from jax import lax
from jax.experimental import pallas as pl
from jax.experimental.pallas import tpu as pltpu
from jax.sharding import PartitionSpec as P


F32 = jnp.float32
BF16 = jnp.bfloat16
I32 = jnp.int32
SUB = 8
BLOCKS = 4
HBM = pl.BlockSpec(memory_space=pl.ANY)
VMEM = pl.BlockSpec(memory_space=pltpu.VMEM)


def dot(left, right, left_dims, right_dims):
    return lax.dot_general(
        left, right, ((left_dims, right_dims), ((), ())), preferred_element_type=F32
    )


def mm(left, right):
    return dot(left, right, (1,), (0,))


def one_hot(hits):
    return jnp.where(hits, 1.0, 0.0).astype(BF16)


def slots_of(ids, axis, experts):
    tok = ids[0].shape[1 - axis]
    shape = (experts, tok) if axis == 0 else (tok, experts)
    expert = lax.broadcasted_iota(I32, shape, axis)
    named = [ids[k] == expert for k in range(2)]
    either = one_hot(named[0] | named[1])
    row = lax.broadcasted_iota(I32, (tok, tok), axis)
    other = lax.broadcasted_iota(I32, (tok, tok), 1 - axis)
    ahead = one_hot(row < other)
    earlier = mm(either, ahead) if axis == 0 else mm(ahead, either)
    slots = []
    for k in range(2):
        rank = jnp.sum(jnp.where(named[k], earlier, 0.0), axis=axis, keepdims=True).astype(I32)
        slots.append((rank & 1) * (experts * SUB) + ids[k] * SUB + (rank >> 1))
    return slots


def dispatch_kernel(weighted, experts, ids_ref, probs_ref, x_ref, out_ref):
    tok = x_ref.shape[0]
    chunk = out_ref.shape[0] // BLOCKS
    slots = slots_of([ids_ref[k : k + 1, :] for k in range(2)], 0, experts)
    for n in range(BLOCKS):
        spot = lax.broadcasted_iota(I32, (chunk, tok), 0) + n * chunk
        hits = [spot == slots[k] for k in range(2)]
        value = mm(one_hot(hits[0] | hits[1]), x_ref[...])
        if weighted:
            probs = jnp.where(hits[0], probs_ref[0:1, :], 0.0) + jnp.where(
                hits[1], probs_ref[1:2, :], 0.0
            )
            value = value * jnp.sum(probs, axis=1, keepdims=True)
        out_ref[n * chunk : (n + 1) * chunk, :] = value.astype(BF16)


def dispatch(ids_t, probs_t, source, experts, weighted):
    return pl.pallas_call(
        functools.partial(dispatch_kernel, weighted, experts),
        out_shape=jax.ShapeDtypeStruct((2 * experts * SUB, source.shape[1]), BF16),
        in_specs=[VMEM] * 3,
        out_specs=VMEM,
        name="send_grads" if weighted else "send_rows",
    )(ids_t, probs_t, source)


def mix_kernel(ids_ref, probs_ref, back_hbm, out_ref, select_ref, back_ref, sems):
    tok = out_ref.shape[0]
    rows = back_ref.shape[0]
    chunk = rows // BLOCKS
    loads = []
    for n in range(BLOCKS):
        here = pl.ds(n * chunk, chunk)
        loads.append(pltpu.make_async_copy(back_hbm.at[here], back_ref.at[here], sems.at[n]))
        loads[n].start()
    slots = slots_of([ids_ref[:, k : k + 1] for k in range(2)], 1, rows // (2 * SUB))
    sums = [0.0, 0.0]
    for n in range(BLOCKS):
        spot = lax.broadcasted_iota(I32, (tok, chunk), 1) + n * chunk
        hits = [spot == slots[k] for k in range(2)]
        select_ref[:, n * chunk : (n + 1) * chunk] = one_hot(hits[0] | hits[1])
        loads[n].wait()
        part = back_ref[n * chunk : (n + 1) * chunk, :]
        sums = [sums[k] + mm(one_hot(hits[k]), part) for k in range(2)]
    total = sums[0] * probs_ref[:, 0:1] + sums[1] * probs_ref[:, 1:2]
    out_ref[...] = total.astype(BF16)


def mix(ids, probs, back):
    tok = ids.shape[0]
    return pl.pallas_call(
        mix_kernel,
        out_shape=[
            jax.ShapeDtypeStruct((tok, back.shape[1]), BF16),
            jax.ShapeDtypeStruct((tok, back.shape[0]), BF16),
        ],
        in_specs=[VMEM, VMEM, HBM],
        scratch_shapes=[pltpu.VMEM(back.shape, BF16), pltpu.SemaphoreType.DMA((BLOCKS,))],
        name="mix",
    )(ids, probs, back)


def add_kernel(select_ref, back_ref, out_ref):
    out_ref[...] = mm(select_ref[...], back_ref[...]).astype(BF16)


def add_routes(select, back):
    return pl.pallas_call(
        add_kernel,
        out_shape=jax.ShapeDtypeStruct((select.shape[0], back.shape[1]), BF16),
        in_specs=[VMEM, VMEM],
        out_specs=VMEM,
        name="add_routes",
    )(select, back)


def write_halves(value_of, stage_ref, out_hbm, sems):
    copies = []
    for half in range(2):
        stage_ref[half] = value_of(half).astype(BF16)
        copies.append(
            pltpu.make_async_copy(stage_ref.at[half], out_hbm.at[half], sems.at[half])
        )
        copies[half].start()
    for copy in copies:
        copy.wait()


def forward_kernel(
    x_hbm, wg_ref, wu_ref, wd_hbm, gp_ref, up_ref, h_ref, out_hbm,
    x_ref, wd_ref, hidden_ref, stage_ref, x_sem, wd_sem, out_sems,
):
    step = pl.program_id(0)
    block = h_ref.shape[1]
    width = x_ref.shape[2]
    load = pltpu.make_async_copy(wd_hbm, wd_ref, wd_sem)

    @pl.when(step == 0)
    def _():
        fetch = pltpu.make_async_copy(x_hbm, x_ref, x_sem)
        fetch.start()
        load.start()
        fetch.wait()

    def project(w_ref):
        return mm(x_ref[0], w_ref[:width, :]) + mm(x_ref[1], w_ref[width:, :])

    gate_pre = project(wg_ref)
    up_pre = project(wu_ref)
    gp_ref[...] = gate_pre
    up_ref[...] = up_pre
    hidden = (gate_pre * jax.nn.sigmoid(gate_pre) * up_pre).astype(BF16)
    h_ref[...] = hidden
    hidden_ref[:, pl.ds(pl.multiple_of(step * block, block), block)] = hidden

    @pl.when(step == BLOCKS - 1)
    def _():
        load.wait()

        def value_of(half):
            return mm(hidden_ref[...], wd_ref[:, half * width : (half + 1) * width])

        write_halves(value_of, stage_ref, out_hbm, out_sems)


def forward(rows_in, pair_weights, down_weights):
    cores, rows, width = rows_in.shape
    hidden, full = down_weights.shape
    block = hidden // BLOCKS
    cols = pl.BlockSpec((rows, block), lambda i: (0, i))
    return pl.pallas_call(
        forward_kernel,
        grid=(BLOCKS,),
        in_specs=[
            pl.BlockSpec(memory_space=pltpu.HBM),
            pl.BlockSpec((full, block), lambda i: (0, i)),
            pl.BlockSpec((full, block), lambda i: (0, i + BLOCKS)),
            HBM,
        ],
        out_specs=[cols, cols, cols, HBM],
        out_shape=[
            jax.ShapeDtypeStruct((rows, hidden), F32),
            jax.ShapeDtypeStruct((rows, hidden), F32),
            jax.ShapeDtypeStruct((rows, hidden), BF16),
            jax.ShapeDtypeStruct((cores, rows, width), BF16),
        ],
        scratch_shapes=[
            pltpu.VMEM((cores, rows, width), BF16),
            pltpu.VMEM((hidden, full), BF16),
            pltpu.VMEM((rows, hidden), BF16),
            pltpu.VMEM((cores, rows, width), BF16),
            pltpu.SemaphoreType.DMA,
            pltpu.SemaphoreType.DMA,
            pltpu.SemaphoreType.DMA((2,)),
        ],
        name="forward",
    )(rows_in, pair_weights, pair_weights, down_weights)


def backward_kernel(
    g_ref, gp_ref, up_ref, wd_ref, wp_hbm, gg_ref, ug_ref, out_hbm,
    wp_ref, pair_ref, stage_ref, wp_sem, out_sems,
):
    step = pl.program_id(0)
    block = gg_ref.shape[1]
    width = g_ref.shape[2]
    hidden = BLOCKS * block
    load = pltpu.make_async_copy(wp_hbm, wp_ref, wp_sem)

    @pl.when(step == 0)
    def _():
        load.start()

    hidden_grad = dot(g_ref[0], wd_ref[:, :width], (1,), (1,)) + dot(
        g_ref[1], wd_ref[:, width:], (1,), (1,)
    )
    gate_pre = gp_ref[...]
    up_pre = up_ref[...]
    sigma = jax.nn.sigmoid(gate_pre)
    gate_grad = (hidden_grad * up_pre * sigma * (1.0 + gate_pre * (1.0 - sigma))).astype(BF16)
    up_grad = (hidden_grad * gate_pre * sigma).astype(BF16)
    gg_ref[...] = gate_grad
    ug_ref[...] = up_grad
    pair_ref[:, pl.ds(pl.multiple_of(step * block, block), block)] = gate_grad
    pair_ref[:, pl.ds(pl.multiple_of(hidden + step * block, block), block)] = up_grad

    @pl.when(step == BLOCKS - 1)
    def _():
        load.wait()

        def value_of(half):
            return dot(pair_ref[...], wp_ref[half * width : (half + 1) * width, :], (1,), (1,))

        write_halves(value_of, stage_ref, out_hbm, out_sems)


def backward(grads_in, gate_pre, up_pre, pair_weights, down_weights):
    cores, rows, width = grads_in.shape
    hidden, full = down_weights.shape
    block = hidden // BLOCKS
    cols = pl.BlockSpec((rows, block), lambda i: (0, i))
    return pl.pallas_call(
        backward_kernel,
        grid=(BLOCKS,),
        in_specs=[
            pl.BlockSpec((cores, rows, width), lambda i: (0, 0, 0)),
            cols,
            cols,
            pl.BlockSpec((block, full), lambda i: (i, 0)),
            HBM,
        ],
        out_specs=[cols, cols, HBM],
        out_shape=[
            jax.ShapeDtypeStruct((rows, hidden), BF16),
            jax.ShapeDtypeStruct((rows, hidden), BF16),
            jax.ShapeDtypeStruct((cores, rows, width), BF16),
        ],
        scratch_shapes=[
            pltpu.VMEM((full, 2 * hidden), BF16),
            pltpu.VMEM((rows, 2 * hidden), BF16),
            pltpu.VMEM((cores, rows, width), BF16),
            pltpu.SemaphoreType.DMA,
            pltpu.SemaphoreType.DMA((2,)),
        ],
        name="backward",
    )(grads_in, gate_pre, up_pre, down_weights, pair_weights)


def both(mine, other, mine_g, other_g):
    return dot(mine, mine_g, (0,), (0,)) + dot(other, other_g, (0,), (0,))


def pair_grad_kernel(core_ref, x_ref, xp_ref, g_ref, gp_ref, u_ref, up_ref, dg_ref, du_ref):
    dg_ref[...] = both(x_ref[...], xp_ref[...], g_ref[...], gp_ref[...]).astype(BF16)
    du_ref[...] = both(x_ref[...], xp_ref[...], u_ref[...], up_ref[...]).astype(BF16)


def down_grad_kernel(core_ref, h_ref, hp_ref, g_ref, gp_ref, out_ref):
    out_ref[...] = both(h_ref[...], hp_ref[...], g_ref[...], gp_ref[...]).astype(BF16)


def share_call(kernel, core, steps, operands, out_rows, out_cols, outs):
    block = out_rows // steps
    grid_spec = pltpu.PrefetchScalarGridSpec(
        num_scalar_prefetch=1,
        grid=(steps,),
        in_specs=[spec for _, spec in operands],
        out_specs=[pl.BlockSpec((block, out_cols), lambda i, c: (i, 0))] * outs,
    )
    shape = jax.ShapeDtypeStruct((out_rows, out_cols), BF16)
    return pl.pallas_call(kernel, out_shape=[shape] * outs, grid_spec=grid_spec)(
        core, *[value for value, _ in operands]
    )


def pair_grads(core, rows_mine, rows_other, rights):
    cores, rows, width = rows_mine.shape
    half = rights[0].shape[1] // 2
    block = width // 2
    left = pl.BlockSpec((None, rows, block), lambda i, c: (i // 2, 0, i % 2))
    right = pl.BlockSpec((rows, half), lambda i, c: (0, c[0]))
    operands = [(rows_mine, left), (rows_other, left)] + [(value, right) for value in rights]
    return share_call(pair_grad_kernel, core, 2 * cores, operands, cores * width, half, 2)


def down_grads(core, hidden_mine, hidden_other, grads_mine, grads_other):
    _, rows, width = grads_mine.shape
    hidden = hidden_mine.shape[1]
    left = pl.BlockSpec((rows, hidden // 2), lambda i, c: (0, i))
    right = pl.BlockSpec((None, rows, width), lambda i, c: (c[0], 0, 0))
    operands = [
        (hidden_mine, left), (hidden_other, left), (grads_mine, right), (grads_other, right),
    ]
    return share_call(down_grad_kernel, core, 2, operands, hidden, width, 1)[0]


def body(patches, expert_ids, gate_probs, out_grad, w_gate, w_up, w_down):
    width = patches.shape[1]
    experts = lax.axis_size("expert")
    core = lax.axis_index("dp")
    core_id = core.astype(I32)[None]

    def swap(value):
        return lax.ppermute(value, "dp", [(0, 1), (1, 0)])

    def exchange(value):
        return lax.all_to_all(
            value.reshape(2 * experts, SUB, width),
            ("dp", "expert"),
            split_axis=0,
            concat_axis=0,
            tiled=True,
        ).reshape(2, experts * SUB, width)

    def in_order(mine, other):
        return jnp.where(core == 0, mine, other), jnp.where(core == 0, other, mine)

    ids_t = expert_ids.T
    probs_t = gate_probs.T
    rows = exchange(dispatch(ids_t, probs_t, patches, experts, False))
    sent_grads = dispatch(ids_t, probs_t, out_grad, experts, True)
    grads = exchange(sent_grads)

    pair_weights = jnp.concatenate(
        in_order(w_gate[0], swap(w_gate[0])) + in_order(w_up[0], swap(w_up[0])), axis=1
    )
    down_weights = jnp.concatenate(in_order(w_down[0], swap(w_down[0])), axis=1)
    pair_weights, down_weights = lax.optimization_barrier((pair_weights, down_weights))

    gate_pre, up_pre, hidden, expert_out = forward(rows, pair_weights, down_weights)
    back_out = exchange(expert_out)
    gate_grad, up_grad, dx_slots = backward(
        grads, gate_pre, up_pre, pair_weights, down_weights
    )
    back_grad = exchange(dx_slots)

    down_grad = down_grads(core_id, hidden, swap(hidden), grads, swap(grads))
    gate_wgrad, up_wgrad = pair_grads(
        core_id,
        rows,
        swap(rows),
        (gate_grad, swap(gate_grad), up_grad, swap(up_grad)),
    )

    mixed, select = mix(expert_ids, gate_probs, back_out.reshape(-1, width))
    patch_grad = add_routes(select, back_grad.reshape(-1, width))
    return mixed, patch_grad, gate_wgrad[None], up_wgrad[None], down_grad[None]


def solution(mesh):
    in_specs = (
        P("expert", "dp"),
        P("expert", None),
        P("expert", None),
        P("expert", "dp"),
        P("expert", None, "dp"),
        P("expert", None, "dp"),
        P("expert", None, "dp"),
    )
    out_specs = (
        P("expert", "dp"),
        P("expert", "dp"),
        P("expert", None, "dp"),
        P("expert", None, "dp"),
        P("expert", None, "dp"),
    )

    return jax.shard_map(body, mesh=mesh, in_specs=in_specs, out_specs=out_specs, check_vma=False)
```

```python
import functools

import jax
import jax.numpy as jnp
from jax import lax
from jax.experimental import pallas as pl
from jax.experimental.pallas import tpu as pltpu
from jax.sharding import PartitionSpec as P


F32 = jnp.float32
BF16 = jnp.bfloat16
I32 = jnp.int32
SUB = 8
BLOCKS = 4
HBM = pl.BlockSpec(memory_space=pl.ANY)
VMEM = pl.BlockSpec(memory_space=pltpu.VMEM)
GRANT = 64000 * 1024


def dot(left, right, left_dims, right_dims):
    return lax.dot_general(
        left, right, ((left_dims, right_dims), ((), ())), preferred_element_type=F32
    )


def mm(left, right):
    return dot(left, right, (1,), (0,))


def one_hot(hits):
    return jnp.where(hits, 1.0, 0.0).astype(BF16)


def slots_of(ids, axis, experts):
    tok = ids[0].shape[1 - axis]
    shape = (experts, tok) if axis == 0 else (tok, experts)
    expert = lax.broadcasted_iota(I32, shape, axis)
    named = [ids[k] == expert for k in range(2)]
    either = one_hot(named[0] | named[1])
    row = lax.broadcasted_iota(I32, (tok, tok), axis)
    other = lax.broadcasted_iota(I32, (tok, tok), 1 - axis)
    ahead = one_hot(row < other)
    earlier = mm(either, ahead) if axis == 0 else mm(ahead, either)
    slots = []
    for k in range(2):
        rank = jnp.sum(jnp.where(named[k], earlier, 0.0), axis=axis, keepdims=True).astype(I32)
        slots.append((rank & 1) * (experts * SUB) + ids[k] * SUB + (rank >> 1))
    return slots


def dispatch_kernel(experts, ids_ref, x_ref, *refs):
    weighted = len(refs) == 4
    out_hbm, out_ref, sems = refs[-3:]
    tok = x_ref.shape[0]
    rows = out_ref.shape[0]
    start = 0
    slots = slots_of([ids_ref[k : k + 1, :] for k in range(2)], 0, experts)
    saves = []
    for n, chunk in enumerate((rows // 2, rows // 4, rows // 8, rows // 8)):
        here = pl.ds(start, chunk)
        spot = lax.broadcasted_iota(I32, (chunk, tok), 0) + start
        hits = [spot == slots[k] for k in range(2)]
        value = mm(one_hot(hits[0] | hits[1]), x_ref[...])
        if weighted:
            probs_ref = refs[0]
            probs = jnp.where(hits[0], probs_ref[0:1, :], 0.0) + jnp.where(
                hits[1], probs_ref[1:2, :], 0.0
            )
            value = value * jnp.sum(probs, axis=1, keepdims=True)
        out_ref[start : start + chunk, :] = value.astype(BF16)
        saves.append(pltpu.make_async_copy(out_ref.at[here], out_hbm.at[here], sems.at[n]))
        saves[n].start()
        start += chunk
    for save in saves:
        save.wait()


def dispatch(experts, ids_t, source, *probs_t):
    rows, width = 2 * experts * SUB, source.shape[1]
    weighted = len(probs_t) == 1
    return pl.pallas_call(
        functools.partial(dispatch_kernel, experts),
        out_shape=jax.ShapeDtypeStruct((rows, width), BF16),
        in_specs=[VMEM] * (2 + len(probs_t)),
        out_specs=HBM,
        scratch_shapes=[pltpu.VMEM((rows, width), BF16), pltpu.SemaphoreType.DMA((BLOCKS,))],
        compiler_params=pltpu.CompilerParams(vmem_limit_bytes=GRANT) if weighted else None,
        name="send_grads" if weighted else "send_rows",
    )(ids_t, source, *probs_t)


def mix_kernel(ids_ref, probs_ref, back_hbm, out_ref, select_ref, back_ref, sems):
    tok = out_ref.shape[0]
    rows = back_ref.shape[0]
    chunk = rows // BLOCKS
    loads = []
    for n in range(BLOCKS):
        here = pl.ds(n * chunk, chunk)
        loads.append(pltpu.make_async_copy(back_hbm.at[here], back_ref.at[here], sems.at[n]))
        loads[n].start()
    slots = slots_of([ids_ref[:, k : k + 1] for k in range(2)], 1, rows // (2 * SUB))
    sums = [0.0, 0.0]
    for n in range(BLOCKS):
        spot = lax.broadcasted_iota(I32, (tok, chunk), 1) + n * chunk
        hits = [spot == slots[k] for k in range(2)]
        select_ref[:, n * chunk : (n + 1) * chunk] = one_hot(hits[0] | hits[1])
        loads[n].wait()
        part = back_ref[n * chunk : (n + 1) * chunk, :]
        sums = [sums[k] + mm(one_hot(hits[k]), part) for k in range(2)]
    total = sums[0] * probs_ref[:, 0:1] + sums[1] * probs_ref[:, 1:2]
    out_ref[...] = total.astype(BF16)


def mix(ids, probs, back):
    tok = ids.shape[0]
    return pl.pallas_call(
        mix_kernel,
        out_shape=[
            jax.ShapeDtypeStruct((tok, back.shape[1]), BF16),
            jax.ShapeDtypeStruct((tok, back.shape[0]), BF16),
        ],
        in_specs=[VMEM, VMEM, HBM],
        scratch_shapes=[pltpu.VMEM(back.shape, BF16), pltpu.SemaphoreType.DMA((BLOCKS,))],
        name="mix",
    )(ids, probs, back)


def write_halves(value_of, stage_ref, out_hbm, sems):
    copies = []
    for half in range(2):
        stage_ref[half] = value_of(half).astype(BF16)
        copies.append(
            pltpu.make_async_copy(stage_ref.at[half], out_hbm.at[half], sems.at[half])
        )
        copies[half].start()
    for copy in copies:
        copy.wait()


def forward_kernel(
    x_hbm, wg_ref, wu_ref, wd_hbm, gp_ref, up_ref, h_ref, out_hbm,
    x_ref, wd_ref, hidden_ref, stage_ref, x_sem, wd_sem, out_sems,
):
    step = pl.program_id(0)
    block = h_ref.shape[1]
    width = x_ref.shape[2]
    load = pltpu.make_async_copy(wd_hbm, wd_ref, wd_sem)

    @pl.when(step == 0)
    def _():
        fetch = pltpu.make_async_copy(x_hbm, x_ref, x_sem)
        fetch.start()
        load.start()
        fetch.wait()

    def project(w_ref):
        return mm(x_ref[0], w_ref[:width, :]) + mm(x_ref[1], w_ref[width:, :])

    gate_pre = project(wg_ref)
    up_pre = project(wu_ref)
    gp_ref[...] = gate_pre
    up_ref[...] = up_pre
    hidden = (gate_pre * jax.nn.sigmoid(gate_pre) * up_pre).astype(BF16)
    h_ref[...] = hidden
    hidden_ref[:, pl.ds(pl.multiple_of(step * block, block), block)] = hidden

    @pl.when(step == BLOCKS - 1)
    def _():
        load.wait()

        def value_of(half):
            return mm(hidden_ref[...], wd_ref[:, half * width : (half + 1) * width])

        write_halves(value_of, stage_ref, out_hbm, out_sems)


def forward(rows_in, pair_weights, down_weights):
    cores, rows, width = rows_in.shape
    hidden, full = down_weights.shape
    block = hidden // BLOCKS
    cols = pl.BlockSpec((rows, block), lambda i: (0, i))
    return pl.pallas_call(
        forward_kernel,
        grid=(BLOCKS,),
        in_specs=[
            pl.BlockSpec(memory_space=pltpu.HBM),
            pl.BlockSpec((full, block), lambda i: (0, i)),
            pl.BlockSpec((full, block), lambda i: (0, i + BLOCKS)),
            HBM,
        ],
        out_specs=[cols, cols, cols, HBM],
        out_shape=[
            jax.ShapeDtypeStruct((rows, hidden), F32),
            jax.ShapeDtypeStruct((rows, hidden), F32),
            jax.ShapeDtypeStruct((rows, hidden), BF16),
            jax.ShapeDtypeStruct((cores, rows, width), BF16),
        ],
        scratch_shapes=[
            pltpu.VMEM((cores, rows, width), BF16),
            pltpu.VMEM((hidden, full), BF16),
            pltpu.VMEM((rows, hidden), BF16),
            pltpu.VMEM((cores, rows, width), BF16),
            pltpu.SemaphoreType.DMA,
            pltpu.SemaphoreType.DMA,
            pltpu.SemaphoreType.DMA((2,)),
        ],
        name="forward",
    )(rows_in, pair_weights, pair_weights, down_weights)


def backward_kernel(
    g_ref, gp_ref, up_ref, wd_ref, wp_hbm, gg_ref, ug_ref, out_hbm,
    wp_ref, pair_ref, stage_ref, wp_sem, out_sems,
):
    step = pl.program_id(0)
    block = gg_ref.shape[1]
    width = g_ref.shape[2]
    hidden = BLOCKS * block
    load = pltpu.make_async_copy(wp_hbm, wp_ref, wp_sem)

    @pl.when(step == 0)
    def _():
        load.start()

    hidden_grad = dot(g_ref[0], wd_ref[:, :width], (1,), (1,)) + dot(
        g_ref[1], wd_ref[:, width:], (1,), (1,)
    )
    gate_pre = gp_ref[...]
    up_pre = up_ref[...]
    sigma = jax.nn.sigmoid(gate_pre)
    gate_grad = (hidden_grad * up_pre * sigma * (1.0 + gate_pre * (1.0 - sigma))).astype(BF16)
    up_grad = (hidden_grad * gate_pre * sigma).astype(BF16)
    gg_ref[...] = gate_grad
    ug_ref[...] = up_grad
    pair_ref[:, pl.ds(pl.multiple_of(step * block, block), block)] = gate_grad
    pair_ref[:, pl.ds(pl.multiple_of(hidden + step * block, block), block)] = up_grad

    @pl.when(step == BLOCKS - 1)
    def _():
        load.wait()

        def value_of(half):
            return dot(pair_ref[...], wp_ref[half * width : (half + 1) * width, :], (1,), (1,))

        write_halves(value_of, stage_ref, out_hbm, out_sems)


def backward(grads_in, gate_pre, up_pre, pair_weights, down_weights):
    cores, rows, width = grads_in.shape
    hidden, full = down_weights.shape
    block = hidden // BLOCKS
    cols = pl.BlockSpec((rows, block), lambda i: (0, i))
    return pl.pallas_call(
        backward_kernel,
        grid=(BLOCKS,),
        in_specs=[
            pl.BlockSpec((cores, rows, width), lambda i: (0, 0, 0)),
            cols,
            cols,
            pl.BlockSpec((block, full), lambda i: (i, 0)),
            HBM,
        ],
        out_specs=[cols, cols, HBM],
        out_shape=[
            jax.ShapeDtypeStruct((rows, hidden), BF16),
            jax.ShapeDtypeStruct((rows, hidden), BF16),
            jax.ShapeDtypeStruct((cores, rows, width), BF16),
        ],
        scratch_shapes=[
            pltpu.VMEM((full, 2 * hidden), BF16),
            pltpu.VMEM((rows, 2 * hidden), BF16),
            pltpu.VMEM((cores, rows, width), BF16),
            pltpu.SemaphoreType.DMA,
            pltpu.SemaphoreType.DMA((2,)),
        ],
        name="backward",
    )(grads_in, gate_pre, up_pre, down_weights, pair_weights)


def both(mine, other, mine_g, other_g):
    return dot(mine, mine_g, (0,), (0,)) + dot(other, other_g, (0,), (0,))


def pair_grad_kernel(core_ref, x_ref, xp_ref, g_ref, gp_ref, u_ref, up_ref, dg_ref, du_ref):
    dg_ref[...] = both(x_ref[...], xp_ref[...], g_ref[...], gp_ref[...]).astype(BF16)
    du_ref[...] = both(x_ref[...], xp_ref[...], u_ref[...], up_ref[...]).astype(BF16)


def down_grad_kernel(core_ref, h_ref, hp_ref, g_ref, gp_ref, out_ref):
    out_ref[...] = both(h_ref[...], hp_ref[...], g_ref[...], gp_ref[...]).astype(BF16)


def share_call(kernel, core, steps, operands, out_rows, out_cols, outs):
    block = out_rows // steps
    grid_spec = pltpu.PrefetchScalarGridSpec(
        num_scalar_prefetch=1,
        grid=(steps,),
        in_specs=[spec for _, spec in operands],
        out_specs=[pl.BlockSpec((block, out_cols), lambda i, c: (i, 0))] * outs,
    )
    shape = jax.ShapeDtypeStruct((out_rows, out_cols), BF16)
    return pl.pallas_call(kernel, out_shape=[shape] * outs, grid_spec=grid_spec)(
        core, *[value for value, _ in operands]
    )


def pair_grads(core, rows_mine, rows_other, rights):
    cores, rows, width = rows_mine.shape
    half = rights[0].shape[1] // 2
    block = width // 2
    left = pl.BlockSpec((None, rows, block), lambda i, c: (i // 2, 0, i % 2))
    right = pl.BlockSpec((rows, half), lambda i, c: (0, c[0]))
    operands = [(rows_mine, left), (rows_other, left)] + [(value, right) for value in rights]
    return share_call(pair_grad_kernel, core, 2 * cores, operands, cores * width, half, 2)


def down_grads(core, hidden_mine, hidden_other, grads_mine, grads_other):
    _, rows, width = grads_mine.shape
    hidden = hidden_mine.shape[1]
    left = pl.BlockSpec((rows, hidden // 2), lambda i, c: (0, i))
    right = pl.BlockSpec((None, rows, width), lambda i, c: (c[0], 0, 0))
    operands = [
        (hidden_mine, left), (hidden_other, left), (grads_mine, right), (grads_other, right),
    ]
    return share_call(down_grad_kernel, core, 2, operands, hidden, width, 1)[0]


def body(patches, expert_ids, gate_probs, out_grad, w_gate, w_up, w_down):
    width = patches.shape[1]
    experts = lax.axis_size("expert")
    core = lax.axis_index("dp")
    core_id = core.astype(I32)[None]

    def swap(value):
        return lax.ppermute(value, "dp", [(0, 1), (1, 0)])

    def exchange(value):
        return lax.all_to_all(
            value.reshape(2 * experts, SUB, width),
            ("dp", "expert"),
            split_axis=0,
            concat_axis=0,
            tiled=True,
        ).reshape(2, experts * SUB, width)

    def in_order(mine, other):
        return jnp.where(core == 0, mine, other), jnp.where(core == 0, other, mine)

    ids_t = expert_ids.T
    probs_t = gate_probs.T
    rows = exchange(dispatch(experts, ids_t, patches))
    sent_grads = dispatch(experts, ids_t, out_grad, probs_t)
    grads = exchange(sent_grads)

    pair_weights = jnp.concatenate(
        in_order(w_gate[0], swap(w_gate[0])) + in_order(w_up[0], swap(w_up[0])), axis=1
    )
    down_weights = jnp.concatenate(in_order(w_down[0], swap(w_down[0])), axis=1)
    pair_weights, down_weights = lax.optimization_barrier((pair_weights, down_weights))

    gate_pre, up_pre, hidden, expert_out = forward(rows, pair_weights, down_weights)
    back_out = exchange(expert_out)
    gate_grad, up_grad, dx_slots = backward(
        grads, gate_pre, up_pre, pair_weights, down_weights
    )
    back_grad = exchange(dx_slots)

    down_grad = down_grads(core_id, hidden, swap(hidden), grads, swap(grads))
    gate_wgrad, up_wgrad = pair_grads(
        core_id,
        rows,
        swap(rows),
        (gate_grad, swap(gate_grad), up_grad, swap(up_grad)),
    )

    mixed, select = mix(expert_ids, gate_probs, back_out.reshape(-1, width))
    patch_grad = mm(select, back_grad.reshape(-1, width)).astype(BF16)
    return mixed, patch_grad, gate_wgrad[None], up_wgrad[None], down_grad[None]


def solution(mesh):
    in_specs = (
        P("expert", "dp"),
        P("expert", None),
        P("expert", None),
        P("expert", "dp"),
        P("expert", None, "dp"),
        P("expert", None, "dp"),
        P("expert", None, "dp"),
    )
    out_specs = (
        P("expert", "dp"),
        P("expert", "dp"),
        P("expert", None, "dp"),
        P("expert", None, "dp"),
        P("expert", None, "dp"),
    )

    return jax.shard_map(body, mesh=mesh, in_specs=in_specs, out_specs=out_specs, check_vma=False)
```

```python
import functools

import jax
import jax.numpy as jnp
from jax import lax
from jax.experimental import pallas as pl
from jax.experimental.pallas import tpu as pltpu
from jax.sharding import PartitionSpec as P


F32 = jnp.float32
BF16 = jnp.bfloat16
I32 = jnp.int32
SUB = 8
BLOCKS = 4
HBM = pl.BlockSpec(memory_space=pl.ANY)
VMEM = pl.BlockSpec(memory_space=pltpu.VMEM)
GRANT = 64000 * 1024


def dot(left, right, left_dims, right_dims):
    return lax.dot_general(
        left, right, ((left_dims, right_dims), ((), ())), preferred_element_type=F32
    )


def mm(left, right):
    return dot(left, right, (1,), (0,))


def one_hot(hits):
    return jnp.where(hits, 1.0, 0.0).astype(BF16)


def slots_of(ids, axis, experts):
    tok = ids[0].shape[1 - axis]
    shape = (experts, tok) if axis == 0 else (tok, experts)
    expert = lax.broadcasted_iota(I32, shape, axis)
    named = [ids[k] == expert for k in range(2)]
    either = one_hot(named[0] | named[1])
    row = lax.broadcasted_iota(I32, (tok, tok), axis)
    other = lax.broadcasted_iota(I32, (tok, tok), 1 - axis)
    ahead = one_hot(row < other)
    earlier = mm(either, ahead) if axis == 0 else mm(ahead, either)
    slots = []
    for k in range(2):
        rank = jnp.sum(jnp.where(named[k], earlier, 0.0), axis=axis, keepdims=True).astype(I32)
        slots.append((rank & 1) * (experts * SUB) + ids[k] * SUB + (rank >> 1))
    return slots


def dispatch_kernel(weighted, experts, ids_ref, probs_ref, x_ref, out_hbm, out_ref, sems):
    tok = x_ref.shape[0]
    chunk = out_ref.shape[0] // BLOCKS
    slots = slots_of([ids_ref[k : k + 1, :] for k in range(2)], 0, experts)
    saves = []
    for n in range(BLOCKS):
        here = pl.ds(n * chunk, chunk)
        spot = lax.broadcasted_iota(I32, (chunk, tok), 0) + n * chunk
        hits = [spot == slots[k] for k in range(2)]
        value = mm(one_hot(hits[0] | hits[1]), x_ref[...])
        if weighted:
            probs = jnp.where(hits[0], probs_ref[0:1, :], 0.0) + jnp.where(
                hits[1], probs_ref[1:2, :], 0.0
            )
            value = value * jnp.sum(probs, axis=1, keepdims=True)
        out_ref[n * chunk : (n + 1) * chunk, :] = value.astype(BF16)
        saves.append(pltpu.make_async_copy(out_ref.at[here], out_hbm.at[here], sems.at[n]))
        saves[n].start()
    for save in saves:
        save.wait()


def dispatch(ids_t, probs_t, source, experts, weighted):
    rows, width = 2 * experts * SUB, source.shape[1]
    return pl.pallas_call(
        functools.partial(dispatch_kernel, weighted, experts),
        out_shape=jax.ShapeDtypeStruct((rows, width), BF16),
        in_specs=[VMEM] * 3,
        out_specs=HBM,
        scratch_shapes=[pltpu.VMEM((rows, width), BF16), pltpu.SemaphoreType.DMA((BLOCKS,))],
        compiler_params=pltpu.CompilerParams(vmem_limit_bytes=GRANT) if weighted else None,
        name="send_grads" if weighted else "send_rows",
    )(ids_t, probs_t, source)


def mix_kernel(ids_ref, probs_ref, back_hbm, out_ref, select_ref, back_ref, sems):
    tok = out_ref.shape[0]
    rows = back_ref.shape[0]
    chunk = rows // BLOCKS
    loads = []
    for n in range(BLOCKS):
        here = pl.ds(n * chunk, chunk)
        loads.append(pltpu.make_async_copy(back_hbm.at[here], back_ref.at[here], sems.at[n]))
        loads[n].start()
    slots = slots_of([ids_ref[:, k : k + 1] for k in range(2)], 1, rows // (2 * SUB))
    sums = [0.0, 0.0]
    for n in range(BLOCKS):
        spot = lax.broadcasted_iota(I32, (tok, chunk), 1) + n * chunk
        hits = [spot == slots[k] for k in range(2)]
        select_ref[:, n * chunk : (n + 1) * chunk] = one_hot(hits[0] | hits[1])
        loads[n].wait()
        part = back_ref[n * chunk : (n + 1) * chunk, :]
        sums = [sums[k] + mm(one_hot(hits[k]), part) for k in range(2)]
    total = sums[0] * probs_ref[:, 0:1] + sums[1] * probs_ref[:, 1:2]
    out_ref[...] = total.astype(BF16)


def mix(ids, probs, back):
    tok = ids.shape[0]
    return pl.pallas_call(
        mix_kernel,
        out_shape=[
            jax.ShapeDtypeStruct((tok, back.shape[1]), BF16),
            jax.ShapeDtypeStruct((tok, back.shape[0]), BF16),
        ],
        in_specs=[VMEM, VMEM, HBM],
        scratch_shapes=[pltpu.VMEM(back.shape, BF16), pltpu.SemaphoreType.DMA((BLOCKS,))],
        name="mix",
    )(ids, probs, back)


def add_kernel(select_ref, back_ref, out_ref):
    out_ref[...] = mm(select_ref[...], back_ref[...]).astype(BF16)


def add_routes(select, back):
    return pl.pallas_call(
        add_kernel,
        out_shape=jax.ShapeDtypeStruct((select.shape[0], back.shape[1]), BF16),
        in_specs=[VMEM, VMEM],
        out_specs=VMEM,
        name="add_routes",
    )(select, back)


def write_halves(value_of, stage_ref, out_hbm, sems):
    copies = []
    for half in range(2):
        stage_ref[half] = value_of(half).astype(BF16)
        copies.append(
            pltpu.make_async_copy(stage_ref.at[half], out_hbm.at[half], sems.at[half])
        )
        copies[half].start()
    for copy in copies:
        copy.wait()


def forward_kernel(
    x_hbm, wg_ref, wu_ref, wd_hbm, gp_ref, up_ref, h_ref, out_hbm,
    x_ref, wd_ref, hidden_ref, stage_ref, x_sem, wd_sem, out_sems,
):
    step = pl.program_id(0)
    block = h_ref.shape[1]
    width = x_ref.shape[2]
    load = pltpu.make_async_copy(wd_hbm, wd_ref, wd_sem)

    @pl.when(step == 0)
    def _():
        fetch = pltpu.make_async_copy(x_hbm, x_ref, x_sem)
        fetch.start()
        load.start()
        fetch.wait()

    def project(w_ref):
        return mm(x_ref[0], w_ref[:width, :]) + mm(x_ref[1], w_ref[width:, :])

    gate_pre = project(wg_ref)
    up_pre = project(wu_ref)
    gp_ref[...] = gate_pre
    up_ref[...] = up_pre
    hidden = (gate_pre * jax.nn.sigmoid(gate_pre) * up_pre).astype(BF16)
    h_ref[...] = hidden
    hidden_ref[:, pl.ds(pl.multiple_of(step * block, block), block)] = hidden

    @pl.when(step == BLOCKS - 1)
    def _():
        load.wait()

        def value_of(half):
            return mm(hidden_ref[...], wd_ref[:, half * width : (half + 1) * width])

        write_halves(value_of, stage_ref, out_hbm, out_sems)


def forward(rows_in, pair_weights, down_weights):
    cores, rows, width = rows_in.shape
    hidden, full = down_weights.shape
    block = hidden // BLOCKS
    cols = pl.BlockSpec((rows, block), lambda i: (0, i))
    return pl.pallas_call(
        forward_kernel,
        grid=(BLOCKS,),
        in_specs=[
            pl.BlockSpec(memory_space=pltpu.HBM),
            pl.BlockSpec((full, block), lambda i: (0, i)),
            pl.BlockSpec((full, block), lambda i: (0, i + BLOCKS)),
            HBM,
        ],
        out_specs=[cols, cols, cols, HBM],
        out_shape=[
            jax.ShapeDtypeStruct((rows, hidden), F32),
            jax.ShapeDtypeStruct((rows, hidden), F32),
            jax.ShapeDtypeStruct((rows, hidden), BF16),
            jax.ShapeDtypeStruct((cores, rows, width), BF16),
        ],
        scratch_shapes=[
            pltpu.VMEM((cores, rows, width), BF16),
            pltpu.VMEM((hidden, full), BF16),
            pltpu.VMEM((rows, hidden), BF16),
            pltpu.VMEM((cores, rows, width), BF16),
            pltpu.SemaphoreType.DMA,
            pltpu.SemaphoreType.DMA,
            pltpu.SemaphoreType.DMA((2,)),
        ],
        compiler_params=pltpu.CompilerParams(vmem_limit_bytes=GRANT),
        name="forward",
    )(rows_in, pair_weights, pair_weights, down_weights)


def backward_kernel(
    g_ref, gp_ref, up_ref, wd_ref, wp_hbm, gg_ref, ug_ref, out_hbm,
    wp_ref, pair_ref, stage_ref, wp_sem, out_sems,
):
    step = pl.program_id(0)
    block = gg_ref.shape[1]
    width = g_ref.shape[2]
    hidden = BLOCKS * block
    load = pltpu.make_async_copy(wp_hbm, wp_ref, wp_sem)

    @pl.when(step == 0)
    def _():
        load.start()

    hidden_grad = dot(g_ref[0], wd_ref[:, :width], (1,), (1,)) + dot(
        g_ref[1], wd_ref[:, width:], (1,), (1,)
    )
    gate_pre = gp_ref[...]
    up_pre = up_ref[...]
    sigma = jax.nn.sigmoid(gate_pre)
    gate_grad = (hidden_grad * up_pre * sigma * (1.0 + gate_pre * (1.0 - sigma))).astype(BF16)
    up_grad = (hidden_grad * gate_pre * sigma).astype(BF16)
    gg_ref[...] = gate_grad
    ug_ref[...] = up_grad
    pair_ref[:, pl.ds(pl.multiple_of(step * block, block), block)] = gate_grad
    pair_ref[:, pl.ds(pl.multiple_of(hidden + step * block, block), block)] = up_grad

    @pl.when(step == BLOCKS - 1)
    def _():
        load.wait()

        def value_of(half):
            return dot(pair_ref[...], wp_ref[half * width : (half + 1) * width, :], (1,), (1,))

        write_halves(value_of, stage_ref, out_hbm, out_sems)


def backward(grads_in, gate_pre, up_pre, pair_weights, down_weights):
    cores, rows, width = grads_in.shape
    hidden, full = down_weights.shape
    block = hidden // BLOCKS
    cols = pl.BlockSpec((rows, block), lambda i: (0, i))
    return pl.pallas_call(
        backward_kernel,
        grid=(BLOCKS,),
        in_specs=[
            pl.BlockSpec((cores, rows, width), lambda i: (0, 0, 0)),
            cols,
            cols,
            pl.BlockSpec((block, full), lambda i: (i, 0)),
            HBM,
        ],
        out_specs=[cols, cols, HBM],
        out_shape=[
            jax.ShapeDtypeStruct((rows, hidden), BF16),
            jax.ShapeDtypeStruct((rows, hidden), BF16),
            jax.ShapeDtypeStruct((cores, rows, width), BF16),
        ],
        scratch_shapes=[
            pltpu.VMEM((full, 2 * hidden), BF16),
            pltpu.VMEM((rows, 2 * hidden), BF16),
            pltpu.VMEM((cores, rows, width), BF16),
            pltpu.SemaphoreType.DMA,
            pltpu.SemaphoreType.DMA((2,)),
        ],
        name="backward",
    )(grads_in, gate_pre, up_pre, down_weights, pair_weights)


def both(mine, other, mine_g, other_g):
    return dot(mine, mine_g, (0,), (0,)) + dot(other, other_g, (0,), (0,))


def pair_grad_kernel(core_ref, x_ref, xp_ref, g_ref, gp_ref, u_ref, up_ref, dg_ref, du_ref):
    dg_ref[...] = both(x_ref[...], xp_ref[...], g_ref[...], gp_ref[...]).astype(BF16)
    du_ref[...] = both(x_ref[...], xp_ref[...], u_ref[...], up_ref[...]).astype(BF16)


def down_grad_kernel(core_ref, h_ref, hp_ref, g_ref, gp_ref, out_ref):
    out_ref[...] = both(h_ref[...], hp_ref[...], g_ref[...], gp_ref[...]).astype(BF16)


def share_call(kernel, core, steps, operands, out_rows, out_cols, outs):
    block = out_rows // steps
    grid_spec = pltpu.PrefetchScalarGridSpec(
        num_scalar_prefetch=1,
        grid=(steps,),
        in_specs=[spec for _, spec in operands],
        out_specs=[pl.BlockSpec((block, out_cols), lambda i, c: (i, 0))] * outs,
    )
    shape = jax.ShapeDtypeStruct((out_rows, out_cols), BF16)
    return pl.pallas_call(kernel, out_shape=[shape] * outs, grid_spec=grid_spec)(
        core, *[value for value, _ in operands]
    )


def pair_grads(core, rows_mine, rows_other, rights):
    cores, rows, width = rows_mine.shape
    half = rights[0].shape[1] // 2
    block = width // 2
    left = pl.BlockSpec((None, rows, block), lambda i, c: (i // 2, 0, i % 2))
    right = pl.BlockSpec((rows, half), lambda i, c: (0, c[0]))
    operands = [(rows_mine, left), (rows_other, left)] + [(value, right) for value in rights]
    return share_call(pair_grad_kernel, core, 2 * cores, operands, cores * width, half, 2)


def down_grads(core, hidden_mine, hidden_other, grads_mine, grads_other):
    _, rows, width = grads_mine.shape
    hidden = hidden_mine.shape[1]
    left = pl.BlockSpec((rows, hidden // 2), lambda i, c: (0, i))
    right = pl.BlockSpec((None, rows, width), lambda i, c: (c[0], 0, 0))
    operands = [
        (hidden_mine, left), (hidden_other, left), (grads_mine, right), (grads_other, right),
    ]
    return share_call(down_grad_kernel, core, 2, operands, hidden, width, 1)[0]


def body(patches, expert_ids, gate_probs, out_grad, w_gate, w_up, w_down):
    width = patches.shape[1]
    experts = lax.axis_size("expert")
    core = lax.axis_index("dp")
    core_id = core.astype(I32)[None]

    def swap(value):
        return lax.ppermute(value, "dp", [(0, 1), (1, 0)])

    def exchange(value):
        return lax.all_to_all(
            value.reshape(2 * experts, SUB, width),
            ("dp", "expert"),
            split_axis=0,
            concat_axis=0,
            tiled=True,
        ).reshape(2, experts * SUB, width)

    def in_order(mine, other):
        return jnp.where(core == 0, mine, other), jnp.where(core == 0, other, mine)

    ids_t = expert_ids.T
    probs_t = gate_probs.T
    rows = exchange(dispatch(ids_t, probs_t, patches, experts, False))
    sent_grads = dispatch(ids_t, probs_t, out_grad, experts, True)
    grads = exchange(sent_grads)

    pair_weights = jnp.concatenate(
        in_order(w_gate[0], swap(w_gate[0])) + in_order(w_up[0], swap(w_up[0])), axis=1
    )
    down_weights = jnp.concatenate(in_order(w_down[0], swap(w_down[0])), axis=1)
    pair_weights, down_weights = lax.optimization_barrier((pair_weights, down_weights))

    gate_pre, up_pre, hidden, expert_out = forward(rows, pair_weights, down_weights)
    back_out = exchange(expert_out)
    gate_grad, up_grad, dx_slots = backward(
        grads, gate_pre, up_pre, pair_weights, down_weights
    )
    back_grad = exchange(dx_slots)

    down_grad = down_grads(core_id, hidden, swap(hidden), grads, swap(grads))
    gate_wgrad, up_wgrad = pair_grads(
        core_id,
        rows,
        swap(rows),
        (gate_grad, swap(gate_grad), up_grad, swap(up_grad)),
    )

    mixed, select = mix(expert_ids, gate_probs, back_out.reshape(-1, width))
    patch_grad = add_routes(select, back_grad.reshape(-1, width))
    return mixed, patch_grad, gate_wgrad[None], up_wgrad[None], down_grad[None]


def solution(mesh):
    in_specs = (
        P("expert", "dp"),
        P("expert", None),
        P("expert", None),
        P("expert", "dp"),
        P("expert", None, "dp"),
        P("expert", None, "dp"),
        P("expert", None, "dp"),
    )
    out_specs = (
        P("expert", "dp"),
        P("expert", "dp"),
        P("expert", None, "dp"),
        P("expert", None, "dp"),
        P("expert", None, "dp"),
    )

    return jax.shard_map(body, mesh=mesh, in_specs=in_specs, out_specs=out_specs, check_vma=False)
```
